512 devices in a mesh: seq: 64 (over z, x), head: 8 (over y, core).
Axes of the slice: x: 4, y: 4, z: 16, core: 2. Of those that a mesh axis runs over, the one named last changes fastest.
Arguments:
- act: bfloat16 [32768, 4608], P('seq', 'head'), may hold values from -6 to 6
- query_rows: bfloat16 [32768, 2048], P('seq', 'head'), may hold values from -6 to 6
- key_rows: bfloat16 [32768, 1024], P('seq', 'head'), may hold values from -6 to 6
- out_adjoint: bfloat16 [32768, 2048], P('seq', 'head'), may hold values from -0.59765625 to 0.59765625
- basis_input: bfloat16 [4608, 4608], P('seq', 'head'), may hold values from -0.09375 to 0.09375
- basis_grad: bfloat16 [8, 128, 128], P('head'), may hold values from -0.5 to 0.5
- eigvals: bfloat16 [4608, 1024], P('head'), may hold values from 0.0019 to 30.5, as said below
- query_act: bfloat16 [64, 4608], P(None, 'head'), may hold values from -6 to 6
- query_adj: bfloat16 [64, 1024], P(None, 'head'), may hold values from -6 to 6
Outputs:
- influence: float32 [32768], P('seq')
The draws below stay inside these ranges and needn't reach their ends.
Inputs may be any that keep to these rules, and one draw needn't show every extreme that they name: eigvals are positive.
All inputs are finite; a program needn't handle non-finite values.
Results may differ from the reference program's by a relative error of at most 0.018.
Values may be sent and summed in bfloat16 or wider, within the bound.
No kernel may reach another device: no remote copies, remote signals or barrier semaphores. Data moves between devices by JAX's collectives and lax.ppermute only.
A program may use at most 64 MiB of HBM per device.

```python
import math
import jax
import jax.numpy as jnp
from jax import lax

D = 4608
HD = 128
HEADS = 8
QHEADS = 16
WINDOW = 4096
LQ = 64
TOK_DEV = 512
TOKENS = 32768


def draw_eigvals(key, part):
    base_key = jax.random.fold_in(key, 11)
    row_key = jax.random.fold_in(key, 12)
    column_key = jax.random.fold_in(key, 13)
    row_scale = jnp.exp(jax.random.uniform(row_key, (D, 1), jnp.float32, 0.0, math.log(10.0)))
    rising = 1.0 + 2.0 * jnp.arange(D, dtype=jnp.float32)[:, None] / (D - 1)
    column_scale = jnp.exp(jax.random.uniform(column_key, (1, HEADS * HD), jnp.float32, 0.0, math.log(10.0)))
    base_value = jnp.exp(jax.random.uniform(base_key, (D, HEADS * HD), jnp.float32, math.log(0.05), 0.0))
    return (0.1 * base_value * row_scale * rising * column_scale).astype(jnp.bfloat16)


def block_levels(own_key, extent, pieces, least, high):
    def one(position, shards_of):
        draws = jax.random.uniform(jax.random.fold_in(jax.random.fold_in(own_key, 6), position), (shards_of,), jnp.float32, least / len(pieces), high / len(pieces))
        return jnp.repeat(jnp.exp(draws), extent[position] // shards_of).reshape((-1,) + (1,) * (len(extent) - position - 1))

    level = one(*pieces[0])
    for cut in pieces[1:]:
        level = level * one(*cut)
    return level


def gaussian(key, dims, spread, bound, cuts=(), held_as=jnp.bfloat16):
    array = jax.random.normal(key, dims, jnp.float32) * spread
    if len(cuts) > 0:
        array = block_levels(key, dims, cuts, -0.22, 0.18) * array
    return jnp.clip(array, min=-bound, max=bound).astype(held_as)


def setup_inputs(seed: int = 0) -> dict:
    key_of = jax.random.split(jax.random.key(seed), 10)
    act = gaussian(key_of[0], (TOKENS, D), 1.0, 6.0, ((0, 64), (1, 8)))
    query_rows = gaussian(key_of[1], (TOKENS, QHEADS * HD), 1.0, 6.0, ((0, 64), (1, 8)))
    key_rows = gaussian(key_of[2], (TOKENS, HEADS * HD), 1.0, 6.0, ((0, 64), (1, 8)))
    out_adjoint = gaussian(key_of[3], (TOKENS, QHEADS * HD), 0.1, 0.59765625, ((0, 64), (1, 8)))
    basis_input = gaussian(key_of[4], (D, D), D ** -0.5, 0.09375, ((0, 64), (1, 8)))
    basis_grad = gaussian(key_of[5], (HEADS, HD, HD), HD ** -0.5, 0.5, ((0, 8),))
    eigvals = draw_eigvals(jax.random.fold_in(key_of[9], 71), 0)
    query_act = gaussian(key_of[7], (LQ, D), 1.0, 6.0, ((1, 8),))
    query_adj = gaussian(key_of[8], (LQ, HEADS * HD), 1.0, 6.0, ((1, 8),))
    return {"act": act, "query_rows": query_rows, "key_rows": key_rows, "out_adjoint": out_adjoint, "basis_input": basis_input, "basis_grad": basis_grad, "eigvals": eigvals, "query_act": query_act, "query_adj": query_adj}


SCORE_SCALE = 1.0 / 12.0
SOFT_CAP = 50.0
DAMP_FACTOR = 0.1


def rotate_heads(matrix, basis_grad):
    row_count = matrix.shape[0]
    split_heads = matrix.reshape(row_count, HEADS, HD).astype(jnp.float32)
    turned = jnp.einsum("the,hef->thf", split_heads, basis_grad.astype(jnp.float32))
    return turned.reshape(row_count, HEADS * HD).astype(jnp.bfloat16)


def value_adjoints(query_rows, key_rows, out_adjoint):
    key_span = WINDOW // TOK_DEV
    block_count = TOKENS // TOK_DEV
    reach_rows = (key_span + 1) * TOK_DEV
    padded_keys = jnp.concatenate([jnp.zeros((key_span * TOK_DEV, HEADS * HD), key_rows.dtype), key_rows], axis=0)

    def one_block(carry, block):
        start = (block * TOK_DEV).astype(jnp.int32)
        queries = lax.dynamic_slice_in_dim(query_rows, start, TOK_DEV, 0).reshape(TOK_DEV, 2 * HEADS, HD).astype(jnp.float32)
        adjoint = lax.dynamic_slice_in_dim(out_adjoint, start, TOK_DEV, 0).reshape(TOK_DEV, 2 * HEADS, HD).astype(jnp.float32)
        keys_here = lax.dynamic_slice_in_dim(padded_keys, start, reach_rows, 0).reshape(reach_rows, HEADS, HD).astype(jnp.float32)
        keys_wide = jnp.repeat(keys_here, 2, axis=1)
        raw = jnp.einsum("ahd,thd->hat", queries, keys_wide) * SCORE_SCALE
        capped = SOFT_CAP * jnp.tanh(raw / SOFT_CAP)
        query_pos = start + jnp.arange(TOK_DEV, dtype=jnp.int32)
        key_pos = start - key_span * TOK_DEV + jnp.arange(reach_rows, dtype=jnp.int32)
        gap_pos = query_pos[:, None] - key_pos[None, :]
        valid = (key_pos[None, :] >= 0) & (gap_pos >= 0) & (gap_pos < WINDOW)
        weights = jnp.where(valid[None], jnp.exp(capped), jnp.zeros_like(capped))
        probs = (weights / jnp.sum(weights, axis=2, keepdims=True)).astype(jnp.bfloat16)
        partial_value = jnp.einsum("hat,ahd->thd", probs.astype(jnp.float32), adjoint)
        partial_value = jnp.sum(partial_value.reshape(reach_rows, HEADS, 2, HD), axis=2).astype(jnp.bfloat16)
        partial_value = partial_value.reshape(reach_rows, HEADS * HD).astype(jnp.float32)
        current = lax.dynamic_slice_in_dim(carry, start, reach_rows, 0)
        carry = lax.dynamic_update_slice_in_dim(carry, current + partial_value, start, 0)
        return carry, None

    initial = jnp.zeros(((block_count + key_span) * TOK_DEV, HEADS * HD), jnp.float32)
    summed, unused = lax.scan(one_block, initial, jnp.arange(block_count, dtype=jnp.int32))
    return summed[key_span * TOK_DEV:].astype(jnp.bfloat16)


def reference(act, query_rows, key_rows, out_adjoint, basis_input, basis_grad, eigvals, query_act, query_adj):
    value_adjoint = value_adjoints(query_rows, key_rows, out_adjoint)
    turned_tokens = rotate_heads(value_adjoint, basis_grad)
    turned_query = rotate_heads(query_adj, basis_grad)
    rotated_tokens = jnp.dot(act, basis_input, preferred_element_type=jnp.float32).astype(jnp.bfloat16)
    rotated_query = jnp.dot(query_act, basis_input, preferred_element_type=jnp.float32).astype(jnp.bfloat16)
    query_grad = jnp.dot(rotated_query.T, turned_query, preferred_element_type=jnp.float32) / LQ
    damping = DAMP_FACTOR * jnp.sum(eigvals.astype(jnp.float32)) / (D * HEADS * HD)
    scaled = (query_grad / (eigvals.astype(jnp.float32) + damping)).astype(jnp.bfloat16)
    mapped = jnp.dot(rotated_tokens, scaled, preferred_element_type=jnp.float32)
    return jnp.sum(mapped * turned_tokens.astype(jnp.float32), axis=1)
```

```python
import functools

import jax
import jax.numpy as jnp
from jax import lax
from jax.experimental import pallas as pl
from jax.experimental.pallas import tpu as pltpu
from jax.sharding import PartitionSpec as P

WINDOW = 4096
SCORE_SCALE = 1.0 / 12.0
SOFT_CAP = 50.0
DAMP_FACTOR = 0.1
LOG2E = 1.4426950408889634
NX = 4
NC = 4
BF = jnp.bfloat16
F32 = jnp.float32
NT = (((1,), (1,)), ((), ()))
TN = (((0,), (0,)), ((), ()))
INTERPRET = False


def vmem(n):
    return [pl.BlockSpec(memory_space=pltpu.VMEM) for _ in range(n)]


def shift_z(value, by, wrap):
    size = lax.axis_size("seq")
    pairs = [(i, (i + by * NX) % size) for i in range(size) if wrap or 0 <= i + by * NX < size]
    return lax.ppermute(value, "seq", pairs)


def shift_x(value, by):
    size = lax.axis_size("seq")
    pairs = [(i, i // NX * NX + (i % NX + by) % NX) for i in range(size)]
    return lax.ppermute(value, "seq", pairs)


def shift_h(value, to):
    size = lax.axis_size("head")
    return lax.ppermute(value, "head", [(i, to(i, size)) for i in range(size)])


def x_groups():
    size = lax.axis_size("seq")
    return [[z * NX + x for x in range(NX)] for z in range(size // NX)]


def c_groups():
    size = lax.axis_size("seq")
    return [
        [(b * NC + c) * NX + x for c in range(NC)]
        for b in range(size // NX // NC)
        for x in range(NX)
    ]


def attend_kernel(span, s_ref, q_ref, a_ref, z2, z1, z0, p1, p2, p3, own, b1, b2, b3, kbuf, w, tot, adjt):
    rows, hd = z0.shape
    s = s_ref[0]
    pairs = (p1, p2, p3)
    kbuf[0] = z0[...]
    kbuf[4] = z1[...]
    kbuf[8] = z2[...]
    for k in range(1, 4):
        kbuf[k + 4] = pairs[k - 1][0]
        kbuf[k] = pairs[k - 1][1]
    tot[...] = jnp.zeros_like(tot)
    half = rows // 2

    def block(o, mode):
        for piece in range(2):
            lo = piece * half
            keys = kbuf[o, lo : lo + half, :]
            for m in range(2):
                raw = lax.dot_general(
                    keys, q_ref[:, m * hd : (m + 1) * hd], NT, preferred_element_type=F32
                )
                e = jnp.exp2(jnp.tanh(raw * (SCORE_SCALE / SOFT_CAP)) * (SOFT_CAP * LOG2E))
                if mode != 0:
                    key_i = lo + lax.broadcasted_iota(jnp.int32, e.shape, 0)
                    query_i = lax.broadcasted_iota(jnp.int32, e.shape, 1)
                    keep = key_i <= query_i if mode < 0 else key_i > query_i
                    e = jnp.where(keep, e, 0.0)
                tot[m] += jnp.sum(e.reshape(half // 8, 8, rows), axis=0)
                w[o, lo : lo + half, m * rows : (m + 1) * rows] = e.astype(BF)

    block(0, -1)

    def step(o, carry):
        block(o, 0)
        return carry

    lax.fori_loop(1, jnp.minimum(s, span - 1) + 1, step, 0)

    @pl.when(s >= span)
    def _():
        block(span, 1)

    @pl.when(s < span)
    def _():
        def clear(o, carry):
            w[o] = jnp.zeros(w.shape[1:], BF)
            return carry

        lax.fori_loop(s + 1, span + 1, clear, 0)

    for m in range(2):
        inv = 1.0 / jnp.sum(tot[m], axis=0, keepdims=True)
        turned = a_ref[:, m * hd : (m + 1) * hd].astype(F32).T
        adjt[:, m * rows : (m + 1) * rows] = (turned * inv).astype(BF)
    for o in range(span + 1):
        piece = lax.dot_general(w[o], adjt[...], NT, preferred_element_type=F32).astype(BF)
        if o % 4 == 0:
            own[2 - o // 4] = piece
        else:
            (b1, b2, b3)[o % 4 - 1][1 - o // 4] = piece


def attend(s, q, a, keys, pairs, span):
    rows, hd = keys[0].shape
    pair = jax.ShapeDtypeStruct((2, rows, hd), BF)
    return pl.pallas_call(
        functools.partial(attend_kernel, span),
        out_shape=(jax.ShapeDtypeStruct((3, rows, hd), BF), pair, pair, pair),
        in_specs=[pl.BlockSpec(memory_space=pltpu.SMEM)] + vmem(8),
        out_specs=tuple(vmem(4)),
        scratch_shapes=[
            pltpu.VMEM((span + 1, rows, hd), BF),
            pltpu.VMEM((span + 1, rows, 2 * rows), BF),
            pltpu.VMEM((2, 8, rows), F32),
            pltpu.VMEM((hd, 2 * rows), BF),
        ],
        interpret=INTERPRET,
        name="attend",
    )(s, q, a, *keys, *pairs)


def rotate_query_kernel(hd, h_ref, pack, *refs):
    *blocks, out = refs
    acc = None
    for j, block in enumerate(blocks):
        chunk = pack[h_ref[j]][:, hd : hd + block.shape[0]]
        term = jnp.dot(chunk, block[...], preferred_element_type=F32)
        acc = term if acc is None else acc + term
    acc = acc.astype(BF)
    for i in range(out.shape[0]):
        out[i] = acc


def rotate_query(h_index, pack, blocks, hd):
    return pl.pallas_call(
        functools.partial(rotate_query_kernel, hd),
        out_shape=jax.ShapeDtypeStruct((NX, pack.shape[1], blocks[0].shape[1]), BF),
        in_specs=[pl.BlockSpec(memory_space=pltpu.SMEM)] + vmem(1 + len(blocks)),
        out_specs=vmem(1)[0],
        interpret=INTERPRET,
        name="rotate_query",
    )(h_index, pack, *blocks)


def spread_kernel(damp_ref, rq, pack, eig, *refs):
    *blocks, out = refs
    hd = eig.shape[1]
    total = rq[0].astype(F32)
    for i in range(1, rq.shape[0]):
        total = total + rq[i].astype(F32)
    grad = lax.dot_general(
        total.astype(BF), pack[0][:, :hd], TN, preferred_element_type=F32
    ) * (1.0 / rq.shape[1])
    scaled = (grad / (eig[...].astype(F32) + damp_ref[0])).astype(BF)
    for j, block in enumerate(blocks):
        out[0, j] = jnp.dot(block[...], scaled, preferred_element_type=F32).astype(BF)


def spread(damping, rq, pack, eig, blocks, hd):
    heads = pack.shape[0]
    rows, cols = blocks[0].shape
    return pl.pallas_call(
        spread_kernel,
        grid=(heads,),
        out_shape=jax.ShapeDtypeStruct((heads, len(blocks), rows, hd), BF),
        in_specs=[
            pl.BlockSpec(memory_space=pltpu.SMEM),
            pl.BlockSpec(rq.shape, lambda g: (0, 0, 0)),
            pl.BlockSpec((1,) + pack.shape[1:], lambda g: (g, 0, 0)),
            pl.BlockSpec((cols, hd), lambda g: (0, g)),
        ]
        + [pl.BlockSpec((rows, cols), lambda g: (0, 0)) for _ in blocks],
        out_specs=pl.BlockSpec((1, len(blocks), rows, hd), lambda g: (g, 0, 0, 0)),
        interpret=INTERPRET,
        name="spread",
    )(damping, rq, pack, eig, *blocks)


def map_tokens_kernel(i_ref, n_ref, bg_ref, partner, *refs):
    *mine, out = refs
    acc = None
    for i, ref in enumerate(mine):
        term = lax.dot_general(n_ref[i_ref[i]], ref[...], TN, preferred_element_type=F32)
        acc = term if acc is None else acc + term
    for i in range(partner.shape[0]):
        acc = acc + lax.dot_general(
            n_ref[i_ref[len(mine) + i]], partner[i], TN, preferred_element_type=F32
        )
    turned = jnp.dot(bg_ref[...], acc.astype(BF), preferred_element_type=F32)
    out[...] = turned.T


def map_tokens(index, n8, bg, mine, partner):
    cols, rows = mine[0].shape
    hd = bg.shape[0]
    steps = 4 if rows % 512 == 0 else 1
    tile = rows // steps
    return pl.pallas_call(
        map_tokens_kernel,
        grid=(steps,),
        out_shape=jax.ShapeDtypeStruct((rows, hd), F32),
        in_specs=[
            pl.BlockSpec(memory_space=pltpu.SMEM),
            pl.BlockSpec(n8.shape, lambda g: (0, 0, 0)),
            pl.BlockSpec(bg.shape, lambda g: (0, 0)),
            pl.BlockSpec((partner.shape[0], cols, tile), lambda g: (0, 0, g)),
        ]
        + [pl.BlockSpec((cols, tile), lambda g: (0, g)) for _ in mine],
        out_specs=pl.BlockSpec((tile, hd), lambda g: (g, 0)),
        interpret=INTERPRET,
        name="map_tokens",
    )(index, n8, bg, partner, *mine)


def rounded(value):
    return lax.reduce_precision(value, 8, 7)


def on_device(
    act, query_rows, key_rows, out_adjoint, basis_input, basis_grad, eigvals, query_act, query_adj
):
    rows, cols = act.shape
    hd = basis_grad.shape[1]
    heads = lax.axis_size("head")
    n_seq = lax.axis_size("seq")
    n_z = n_seq // NX
    n_m = n_z // NC
    z_per_head = n_z // heads
    kr = basis_input.shape[0]
    lq = query_act.shape[0]
    span = WINDOW // rows
    s = lax.axis_index("seq")
    h = lax.axis_index("head")
    z, x = s >> 2, s & 3
    b = z >> 2

    key_1 = shift_z(key_rows, 1, False)
    key_2 = shift_z(key_rows, 2, False)
    ahead = [x + k < NX for k in range(4)]
    pairs = []
    for k in range(1, 4):
        pair = jnp.stack(
            [jnp.where(ahead[k], key_1, key_2), jnp.where(ahead[k], key_rows, key_1)]
        )
        pairs.append(shift_x(pair, k))

    basis = [basis_input] + [shift_z(basis_input, -NC * j, True) for j in range(1, n_m)]

    n_y = heads // 2
    act_t = act.T
    mine = [act_t] + [shift_h(act_t, lambda i, n, j=j: (i + 2 * j) % n) for j in range(1, n_y)]
    partner = shift_h(jnp.stack(mine), lambda i, n: i ^ 1)

    turned_query = jnp.dot(query_adj, basis_grad[0], preferred_element_type=F32).astype(BF)
    local = jnp.sum(eigvals, dtype=F32)
    high = rounded(local)
    mid = rounded(local - high)
    low = local - high - mid
    parts = jnp.stack([high, mid, low]).astype(BF)
    offset = ((z & (z_per_head - 1)) * NX + x) * kr
    chunk = lax.dynamic_slice_in_dim(query_act, offset, kr, 1)
    pack = jnp.concatenate(
        [
            turned_query,
            chunk,
            jnp.broadcast_to(parts[None], (lq, 3)),
            jnp.zeros((lq, hd - kr - 3), BF),
        ],
        axis=1,
    )
    pack = lax.all_to_all(jnp.broadcast_to(pack[None], (heads,) + pack.shape), "head", 0, 0)
    eigen_total = jnp.sum(pack[:, 0, hd + kr : hd + kr + 3].astype(F32))
    damping = DAMP_FACTOR * eigen_total / (cols * heads * eigvals.shape[1])

    h_index = ((z + NC * jnp.arange(n_m, dtype=jnp.int32)) & (n_z - 1)) // z_per_head
    rq = rotate_query(h_index, pack, basis, hd)
    rq = lax.all_to_all(rq, "seq", 0, 0, axis_index_groups=x_groups())
    rq = jnp.sum(rq.astype(F32), axis=0).astype(BF)
    rq = jnp.broadcast_to(rq[None], (NC,) + rq.shape)
    rq = lax.all_to_all(rq, "seq", 0, 0, axis_index_groups=c_groups())

    n = spread(damping[None], rq, pack, eigvals, basis, hd)
    n = lax.all_to_all(n, "head", 0, 0)
    n = jnp.sum(n.astype(F32), axis=0).astype(BF)
    n = jnp.broadcast_to(n[None], (NC,) + n.shape)
    n = lax.all_to_all(n, "seq", 0, 0, axis_index_groups=c_groups())
    n = jnp.broadcast_to(n[None], (NX,) + n.shape)
    n = lax.all_to_all(n, "seq", 0, 0, axis_index_groups=x_groups())
    n = n.transpose(2, 1, 0, 3, 4).reshape(heads, cols, hd)
    j = jnp.arange(n_y, dtype=jnp.int32)
    order = (h + 2 * (n_y - j)) & (heads - 1)
    order = jnp.concatenate([order, order ^ 1])
    index = 2 * (((order >> 1) - b) & (n_m - 1)) + (order & 1)
    mapped = map_tokens(index, n, basis_grad[0], mine, partner)

    own, *back = attend(
        s[None], query_rows, out_adjoint, (key_2, key_1, key_rows), pairs, span
    )
    own = own.astype(F32)
    sum_0, sum_1, sum_2 = own[2], own[1], own[0]
    for k in range(1, 4):
        got = shift_x(back[k - 1], -k).astype(F32)
        sum_0 = sum_0 + jnp.where(ahead[k], got[1], 0.0)
        sum_1 = sum_1 + jnp.where(ahead[k], got[0], got[1])
        sum_2 = sum_2 + jnp.where(ahead[k], 0.0, got[0])
    got_1 = shift_z(sum_1.astype(BF), -1, False)
    got_2 = shift_z(sum_2.astype(BF), -2, False)
    value_adjoint = sum_0 + got_1.astype(F32) + got_2.astype(F32)
    partial = jnp.sum(mapped * value_adjoint, axis=1)
    partial = jnp.broadcast_to(partial.reshape(1, -1, 128), (heads, rows // 128, 128))
    partial = lax.all_to_all(partial, "head", 0, 0)
    return jnp.sum(partial, axis=0).reshape(rows)


def solution(mesh):
    return jax.shard_map(
        on_device,
        mesh=mesh,
        in_specs=(
            P("seq", "head"),
            P("seq", "head"),
            P("seq", "head"),
            P("seq", "head"),
            P("seq", "head"),
            P("head", None, None),
            P("head", None),
            P(None, "head"),
            P(None, "head"),
        ),
        out_specs=P("seq"),
        check_vma=False,
    )
```

```python
import functools

import jax
import jax.numpy as jnp
from jax import lax
from jax.experimental import pallas as pl
from jax.experimental.pallas import tpu as pltpu
from jax.sharding import PartitionSpec as P

WINDOW = 4096
SCORE_SCALE = 1.0 / 12.0
SOFT_CAP = 50.0
DAMP_FACTOR = 0.1
LOG2E = 1.4426950408889634
NX = 4
NC = 4
BF = jnp.bfloat16
F32 = jnp.float32
NT = (((1,), (1,)), ((), ()))
INTERPRET = False


def vmem(n):
    return [pl.BlockSpec(memory_space=pltpu.VMEM) for _ in range(n)]


def shift_z(value, by, wrap):
    size = lax.axis_size("seq")
    pairs = [(i, (i + by * NX) % size) for i in range(size) if wrap or 0 <= i + by * NX < size]
    return lax.ppermute(value, "seq", pairs)


def x_groups():
    size = lax.axis_size("seq")
    return [[z * NX + x for x in range(NX)] for z in range(size // NX)]


def c_groups():
    size = lax.axis_size("seq")
    return [
        [(b * NC + c) * NX + x for c in range(NC)]
        for b in range(size // NX // NC)
        for x in range(NX)
    ]


def m_groups():
    size = lax.axis_size("seq")
    n_m = size // NX // NC
    return [[(m * NC + c) * NX + x for m in range(n_m)] for c in range(NC) for x in range(NX)]


def exchange(value, axis, groups=None):
    return lax.all_to_all(value, axis, 0, 0, axis_index_groups=groups)


def copies(value, count):
    return jnp.broadcast_to(value[None], (count,) + value.shape)


def attend_kernel(span, s_ref, q_ref, a_ref, far, near, back, last, kbuf, w, tot, adjt):
    rows, hd = far.shape
    s = s_ref[0]
    x = s & (NX - 1)
    kbuf[span] = far[...]
    for source in range(NX):
        k = (x - source) & (NX - 1)
        kbuf[k + NX] = near[source, 0]
        kbuf[k] = near[source, 1]
    tot[...] = jnp.zeros_like(tot)
    half = rows // 2

    def block(o, mode):
        for piece in range(2):
            lo = piece * half
            keys = kbuf[o, lo : lo + half, :]
            for m in range(2):
                raw = lax.dot_general(
                    keys, q_ref[:, m * hd : (m + 1) * hd], NT, preferred_element_type=F32
                )
                e = jnp.exp2(jnp.tanh(raw * (SCORE_SCALE / SOFT_CAP)) * (SOFT_CAP * LOG2E))
                if mode != 0:
                    key_i = lo + lax.broadcasted_iota(jnp.int32, e.shape, 0)
                    query_i = lax.broadcasted_iota(jnp.int32, e.shape, 1)
                    keep = key_i <= query_i if mode < 0 else key_i > query_i
                    e = jnp.where(keep, e, 0.0)
                tot[m] += jnp.sum(e.reshape(half // 8, 8, rows), axis=0)
                w[o, lo : lo + half, m * rows : (m + 1) * rows] = e.astype(BF)

    block(0, -1)

    def step(o, carry):
        block(o, 0)
        return carry

    lax.fori_loop(1, jnp.minimum(s, span - 1) + 1, step, 0)

    @pl.when(s >= span)
    def _():
        block(span, 1)

    @pl.when(s < span)
    def _():
        def clear(o, carry):
            w[o] = jnp.zeros(w.shape[1:], BF)
            return carry

        lax.fori_loop(s + 1, span + 1, clear, 0)

    for m in range(2):
        inv = 1.0 / jnp.sum(tot[m], axis=0, keepdims=True)
        turned = a_ref[:, m * hd : (m + 1) * hd].astype(F32).T
        adjt[:, m * rows : (m + 1) * rows] = (turned * inv).astype(BF)
    for o in range(span + 1):
        piece = lax.dot_general(w[o], adjt[...], NT, preferred_element_type=F32).astype(BF)
        if o == span:
            last[...] = piece
        else:
            back[(x - o) & (NX - 1), 1 - o // NX] = piece


def attend(s, q, a, far, near, span):
    rows, hd = far.shape
    return pl.pallas_call(
        functools.partial(attend_kernel, span),
        out_shape=(jax.ShapeDtypeStruct(near.shape, BF), jax.ShapeDtypeStruct(far.shape, BF)),
        in_specs=[pl.BlockSpec(memory_space=pltpu.SMEM)] + vmem(4),
        out_specs=tuple(vmem(2)),
        scratch_shapes=[
            pltpu.VMEM((span + 1, rows, hd), BF),
            pltpu.VMEM((span + 1, rows, 2 * rows), BF),
            pltpu.VMEM((2, 8, rows), F32),
            pltpu.VMEM((hd, 2 * rows), BF),
        ],
        interpret=INTERPRET,
        name="attend",
    )(s, q, a, far, near)


def pack_kernel(at_ref, act, adj, bg, eig, out):
    lq, hd = adj.shape
    heads = out.shape[0]
    kr = act.shape[1] // heads
    turned = jnp.dot(adj[...], bg[...], preferred_element_type=F32).astype(BF)
    total = jnp.sum(jnp.sum(eig[...].astype(F32), axis=0, keepdims=True), axis=1, keepdims=True)
    high = total.astype(BF).astype(F32)
    mid = (total - high).astype(BF).astype(F32)
    low = total - high - mid
    lane = lax.broadcasted_iota(jnp.int32, (lq, hd - kr), 1)
    tail = jnp.where(lane == 0, high, jnp.where(lane == 1, mid, jnp.where(lane == 2, low, 0.0)))
    out[0, :, :hd] = turned
    out[0, :, hd + kr :] = tail.astype(BF)
    for i in range(heads):

        @pl.when(at_ref[0] == i)
        def _():
            out[0, :, hd : hd + kr] = act[:, i * kr : (i + 1) * kr]

    for i in range(1, heads):
        out[i] = out[0]


def pack_query(at, act, adj, bg, eig, heads):
    lq, hd = adj.shape
    return pl.pallas_call(
        pack_kernel,
        out_shape=jax.ShapeDtypeStruct((heads, lq, 2 * hd), BF),
        in_specs=[pl.BlockSpec(memory_space=pltpu.SMEM)] + vmem(4),
        out_specs=vmem(1)[0],
        interpret=INTERPRET,
        name="pack_query",
    )(at, act, adj, bg, eig)


def rotate_query_kernel(hd, c_ref, pack, basis, out):
    kr = basis.shape[1]
    acc = None
    for m in range(basis.shape[0]):
        chunk = pack[2 * m + (c_ref[0] >> 1)][:, hd : hd + kr]
        term = jnp.dot(chunk, basis[m], preferred_element_type=F32)
        acc = term if acc is None else acc + term
    acc = acc.astype(BF)
    for i in range(out.shape[0]):
        out[i] = acc


def rotate_query(c, pack, basis, hd):
    return pl.pallas_call(
        functools.partial(rotate_query_kernel, hd),
        out_shape=jax.ShapeDtypeStruct((NX, pack.shape[1], basis.shape[2]), BF),
        in_specs=[pl.BlockSpec(memory_space=pltpu.SMEM)] + vmem(2),
        out_specs=vmem(1)[0],
        interpret=INTERPRET,
        name="rotate_query",
    )(c, pack, basis)


def spread_kernel(count, rq, pack, eig, basis, out, rq_t):
    hd = eig.shape[1]
    kr = basis.shape[1]
    g = pl.program_id(0)

    @pl.when(g == 0)
    def _():
        total = rq[0].astype(F32)
        for i in range(1, rq.shape[0]):
            total = total + rq[i].astype(F32)
        rq_t[...] = total.T.astype(BF)

    sums = pack[:, 0:1, hd + kr : hd + kr + 3].astype(F32)
    damping = jnp.sum(jnp.sum(sums, axis=0), axis=1, keepdims=True) * (DAMP_FACTOR / count)
    turned = pack[g][:, :hd]
    grad = jnp.dot(rq_t[...], turned, preferred_element_type=F32) * (1.0 / rq.shape[1])
    scaled = (grad / (eig[...].astype(F32) + damping)).astype(BF)
    for m in range(basis.shape[0]):
        out[0, m] = jnp.dot(basis[m], scaled, preferred_element_type=F32).astype(BF)


def spread(count, rq, pack, eig, basis, hd):
    heads = pack.shape[0]
    n_m, rows, cols = basis.shape
    return pl.pallas_call(
        functools.partial(spread_kernel, count),
        grid=(heads,),
        out_shape=jax.ShapeDtypeStruct((heads, n_m, rows, hd), BF),
        in_specs=[
            pl.BlockSpec(rq.shape, lambda g: (0, 0, 0)),
            pl.BlockSpec(pack.shape, lambda g: (0, 0, 0)),
            pl.BlockSpec((cols, hd), lambda g: (0, g)),
            pl.BlockSpec(basis.shape, lambda g: (0, 0, 0)),
        ],
        out_specs=pl.BlockSpec((1, n_m, rows, hd), lambda g: (g, 0, 0, 0)),
        scratch_shapes=[pltpu.VMEM((cols, rq.shape[1]), BF)],
        interpret=INTERPRET,
        name="spread",
    )(rq, pack, eig, basis)


def map_tokens_kernel(core_ref, n_ref, bg_ref, mine, partner, out, n_t):
    @pl.when(pl.program_id(0) == 0)
    def _():
        for g in range(n_ref.shape[0]):
            n_t[g] = n_ref[g].T

    acc = None
    for y in range(mine.shape[0]):
        for core, ref in ((core_ref[0], mine), (1 - core_ref[0], partner)):
            term = jnp.dot(n_t[2 * y + core], ref[y], preferred_element_type=F32)
            acc = term if acc is None else acc + term
    turned = jnp.dot(bg_ref[...], acc.astype(BF), preferred_element_type=F32)
    out[...] = turned.T


def map_tokens(core, n8, bg, mine, partner):
    n_y, cols, rows = mine.shape
    hd = bg.shape[0]
    steps = 4 if rows % 512 == 0 else 1
    tile = rows // steps
    return pl.pallas_call(
        map_tokens_kernel,
        grid=(steps,),
        out_shape=jax.ShapeDtypeStruct((rows, hd), F32),
        in_specs=[
            pl.BlockSpec(memory_space=pltpu.SMEM),
            pl.BlockSpec(n8.shape, lambda g: (0, 0, 0)),
            pl.BlockSpec(bg.shape, lambda g: (0, 0)),
            pl.BlockSpec((n_y, cols, tile), lambda g: (0, 0, g)),
            pl.BlockSpec((n_y, cols, tile), lambda g: (0, 0, g)),
        ],
        out_specs=pl.BlockSpec((tile, hd), lambda g: (g, 0)),
        scratch_shapes=[pltpu.VMEM((n8.shape[0], hd, cols), BF)],
        interpret=INTERPRET,
        name="map_tokens",
    )(core, n8, bg, mine, partner)


def on_device(
    act, query_rows, key_rows, out_adjoint, basis_input, basis_grad, eigvals, query_act, query_adj
):
    rows, cols = act.shape
    hd = basis_grad.shape[1]
    heads = lax.axis_size("head")
    n_m = lax.axis_size("seq") // NX // NC
    kr = basis_input.shape[0]
    span = WINDOW // rows
    s = lax.axis_index("seq")
    x = s & (NX - 1)
    c = (s >> 2) & (NC - 1)
    core = lax.axis_index("head") & 1
    ahead = jnp.arange(NX, dtype=jnp.int32) >= x

    key_1 = shift_z(key_rows, 1, False)
    key_2 = shift_z(key_rows, 2, False)
    basis = exchange(copies(basis_input, n_m), "seq", m_groups())
    at = (c & 1) * NX + x
    pack = pack_query(at[None], query_act, query_adj, basis_grad[0], eigvals, heads)
    pack = exchange(pack, "head")
    act_y = copies(act.T, heads // 2)
    act_y = exchange(act_y, "head", [list(range(k, heads, 2)) for k in range(2)])

    keys = jnp.where(
        ahead[:, None, None, None],
        jnp.stack([key_1, key_rows])[None],
        jnp.stack([key_2, key_1])[None],
    )
    keys, pack, basis = lax.optimization_barrier((keys, pack, basis))
    keys = exchange(keys, "seq", x_groups())
    rq = rotate_query(c[None], pack, basis, hd)
    rq = exchange(rq, "seq", x_groups())
    rq = copies(jnp.sum(rq.astype(F32), axis=0).astype(BF), NC)
    keys, rq = lax.optimization_barrier((keys, rq))

    rq = exchange(rq, "seq", c_groups())
    back, far = attend(s[None], query_rows, out_adjoint, key_2, keys, span)
    back, far, rq, act_y = lax.optimization_barrier((back, far, rq, act_y))

    back = exchange(back, "seq", x_groups())
    n = spread(float(cols * heads * eigvals.shape[1]), rq, pack, eigvals, basis, hd)
    n = exchange(n, "head")
    partner = lax.ppermute(act_y, "head", [(i, i ^ 1) for i in range(heads)])
    back = back.astype(F32)
    sum_0, sum_1, sum_2 = 0.0, 0.0, far.astype(F32)
    for source in range(NX):
        later = ahead[source]
        sum_0 = sum_0 + jnp.where(later, back[source, 1], 0.0)
        sum_1 = sum_1 + jnp.where(later, back[source, 0], back[source, 1])
        sum_2 = sum_2 + jnp.where(later, 0.0, back[source, 0])
    n = copies(jnp.sum(n.astype(F32), axis=0).astype(BF), NC)
    sum_0, sum_1, sum_2, n = lax.optimization_barrier(
        (sum_0, sum_1.astype(BF), sum_2.astype(BF), n)
    )

    got_1 = shift_z(sum_1, -1, False)
    got_2 = shift_z(sum_2, -2, False)
    n = copies(exchange(n, "seq", c_groups()), NX)
    n = exchange(n, "seq", x_groups())
    n = n.transpose(2, 1, 0, 3, 4).reshape(heads, cols, hd)
    mapped = map_tokens(core[None], n, basis_grad[0], act_y, partner)
    value_adjoint = sum_0 + got_1.astype(F32) + got_2.astype(F32)
    partial = jnp.sum(mapped * value_adjoint, axis=1)
    partial = exchange(copies(partial.reshape(rows // 128, 128), heads), "head")
    return jnp.sum(partial, axis=0).reshape(rows)


def solution(mesh):
    return jax.shard_map(
        on_device,
        mesh=mesh,
        in_specs=(
            P("seq", "head"),
            P("seq", "head"),
            P("seq", "head"),
            P("seq", "head"),
            P("seq", "head"),
            P("head", None, None),
            P("head", None),
            P(None, "head"),
            P(None, "head"),
        ),
        out_specs=P("seq"),
        check_vma=False,
    )
```

```python
import functools

import jax
import jax.numpy as jnp
from jax import lax
from jax.experimental import pallas as pl
from jax.experimental.pallas import tpu as pltpu
from jax.sharding import PartitionSpec as P


WINDOW = 4096
SCORE_SCALE = 1.0 / 12.0
SOFT_CAP = 50.0
DAMP_FACTOR = 0.1
LOG2E = 1.4426950408889634
NX = 4
NC = 4
BF = jnp.bfloat16
F32 = jnp.float32
NT = (((1,), (1,)), ((), ()))
INTERPRET = False


def vmem(n):
    return [pl.BlockSpec(memory_space=pltpu.VMEM) for _ in range(n)]


def held(values):
    return [pltpu.with_memory_space_constraint(v, pltpu.VMEM) for v in values]


def limit(mib):
    return pltpu.CompilerParams(vmem_limit_bytes=mib << 20)


def shift_z(value, by, wrap):
    size = lax.axis_size("seq")
    pairs = [(i, (i + by * NX) % size) for i in range(size) if wrap or 0 <= i + by * NX < size]
    return lax.ppermute(value, "seq", pairs)


def shift_x(value, by):
    size = lax.axis_size("seq")
    pairs = [(i, i // NX * NX + (i % NX + by) % NX) for i in range(size)]
    return lax.ppermute(value, "seq", pairs)


def shift_y(value, by):
    size = lax.axis_size("head")
    return lax.ppermute(value, "head", [(i, (i + 2 * by) % size) for i in range(size)])


def x_groups():
    size = lax.axis_size("seq")
    return [[z * NX + x for x in range(NX)] for z in range(size // NX)]


def c_groups():
    size = lax.axis_size("seq")
    return [
        [(b * NC + c) * NX + x for c in range(NC)]
        for b in range(size // NX // NC)
        for x in range(NX)
    ]


def m_groups():
    size = lax.axis_size("seq")
    n_m = size // NX // NC
    return [[(m * NC + c) * NX + x for m in range(n_m)] for c in range(NC) for x in range(NX)]


def exchange(value, axis, groups=None):
    return lax.all_to_all(value, axis, 0, 0, axis_index_groups=groups)


def copies(value, count):
    return jnp.broadcast_to(value[None], (count,) + value.shape)


def attend_kernel(span, s_ref, q_ref, a_ref, z2, z1, z0, p1, p2, p3, own, b1, b2, b3, kbuf, w, tot, adjt):
    rows, hd = z0.shape
    s = s_ref[0]
    pairs = (p1, p2, p3)
    kbuf[0] = z0[...]
    kbuf[4] = z1[...]
    kbuf[8] = z2[...]
    for k in range(1, 4):
        kbuf[k + 4] = pairs[k - 1][0]
        kbuf[k] = pairs[k - 1][1]
    tot[...] = jnp.zeros_like(tot)
    half = rows // 2

    def block(o, mode):
        for piece in range(2):
            lo = piece * half
            keys = kbuf[o, lo : lo + half, :]
            for m in range(2):
                raw = lax.dot_general(
                    keys, q_ref[:, m * hd : (m + 1) * hd], NT, preferred_element_type=F32
                )
                e = jnp.exp2(jnp.tanh(raw * (SCORE_SCALE / SOFT_CAP)) * (SOFT_CAP * LOG2E))
                if mode != 0:
                    key_i = lo + lax.broadcasted_iota(jnp.int32, e.shape, 0)
                    query_i = lax.broadcasted_iota(jnp.int32, e.shape, 1)
                    keep = key_i <= query_i if mode < 0 else key_i > query_i
                    e = jnp.where(keep, e, 0.0)
                tot[m] += jnp.sum(e.reshape(half // 8, 8, rows), axis=0)
                w[o, lo : lo + half, m * rows : (m + 1) * rows] = e.astype(BF)

    block(0, -1)

    def step(o, carry):
        block(o, 0)
        return carry

    lax.fori_loop(1, jnp.minimum(s, span - 1) + 1, step, 0)

    @pl.when(s >= span)
    def _():
        block(span, 1)

    @pl.when(s < span)
    def _():
        def clear(o, carry):
            w[o] = jnp.zeros(w.shape[1:], BF)
            return carry

        lax.fori_loop(s + 1, span + 1, clear, 0)

    for m in range(2):
        inv = 1.0 / jnp.sum(tot[m], axis=0, keepdims=True)
        turned = a_ref[:, m * hd : (m + 1) * hd].astype(F32).T
        adjt[:, m * rows : (m + 1) * rows] = (turned * inv).astype(BF)
    for o in range(span + 1):
        piece = lax.dot_general(w[o], adjt[...], NT, preferred_element_type=F32).astype(BF)
        if o % 4 == 0:
            own[2 - o // 4] = piece
        else:
            (b1, b2, b3)[o % 4 - 1][1 - o // 4] = piece


def attend(s, q, a, keys, pairs, span):
    rows, hd = keys[0].shape
    pair = jax.ShapeDtypeStruct((2, rows, hd), BF)
    return pl.pallas_call(
        functools.partial(attend_kernel, span),
        out_shape=(jax.ShapeDtypeStruct((3, rows, hd), BF), pair, pair, pair),
        in_specs=[pl.BlockSpec(memory_space=pltpu.SMEM)] + vmem(8),
        out_specs=tuple(vmem(4)),
        scratch_shapes=[
            pltpu.VMEM((span + 1, rows, hd), BF),
            pltpu.VMEM((span + 1, rows, 2 * rows), BF),
            pltpu.VMEM((2, 8, rows), F32),
            pltpu.VMEM((hd, 2 * rows), BF),
        ],
        interpret=INTERPRET,
        name="attend",
        compiler_params=limit(24),
    )(s, q, a, *held([*keys, *pairs]))


def pack_kernel(at_ref, act, adj, bg, eig, out):
    lq, hd = adj.shape
    heads = out.shape[0]
    kr = act.shape[1] // heads
    turned = jnp.dot(adj[...], bg[...], preferred_element_type=F32).astype(BF)
    total = jnp.sum(jnp.sum(eig[...].astype(F32), axis=0, keepdims=True), axis=1, keepdims=True)
    high = total.astype(BF).astype(F32)
    mid = (total - high).astype(BF).astype(F32)
    low = total - high - mid
    lane = lax.broadcasted_iota(jnp.int32, (lq, hd - kr), 1)
    tail = jnp.where(lane == 0, high, jnp.where(lane == 1, mid, jnp.where(lane == 2, low, 0.0)))
    out[0, :, :hd] = turned
    out[0, :, hd + kr :] = tail.astype(BF)
    for i in range(heads):

        @pl.when(at_ref[0] == i)
        def _():
            out[0, :, hd : hd + kr] = act[:, i * kr : (i + 1) * kr]

    for i in range(1, heads):
        out[i] = out[0]


def pack_query(at, act, adj, bg, eig, heads):
    lq, hd = adj.shape
    return pl.pallas_call(
        pack_kernel,
        out_shape=jax.ShapeDtypeStruct((heads, lq, 2 * hd), BF),
        in_specs=[pl.BlockSpec(memory_space=pltpu.SMEM)] + vmem(4),
        out_specs=vmem(1)[0],
        interpret=INTERPRET,
        name="pack_query",
        compiler_params=limit(16),
    )(at, act, adj, bg, eig)


def rotate_query_kernel(hd, c_ref, pack, basis, out):
    kr = basis.shape[1]
    acc = None
    for m in range(basis.shape[0]):
        chunk = pack[2 * m + (c_ref[0] >> 1)][:, hd : hd + kr]
        term = jnp.dot(chunk, basis[m], preferred_element_type=F32)
        acc = term if acc is None else acc + term
    acc = acc.astype(BF)
    for i in range(out.shape[0]):
        out[i] = acc


def rotate_query(c, pack, basis, hd):
    return pl.pallas_call(
        functools.partial(rotate_query_kernel, hd),
        out_shape=jax.ShapeDtypeStruct((NX, pack.shape[1], basis.shape[2]), BF),
        in_specs=[pl.BlockSpec(memory_space=pltpu.SMEM)] + vmem(2),
        out_specs=vmem(1)[0],
        interpret=INTERPRET,
        name="rotate_query",
        compiler_params=limit(16),
    )(c, *held([pack, basis]))


def spread_kernel(count, rq, pack, eig, basis, out, rq_t, rows_all, scaled):
    hd = out.shape[3]
    n_m, kr, _ = basis.shape
    per = out.shape[0]
    g = pl.program_id(0)

    @pl.when(g == 0)
    def _():
        total = rq[0].astype(F32)
        for i in range(1, rq.shape[0]):
            total = total + rq[i].astype(F32)
        rq_t[...] = total.T.astype(BF)
        for m in range(n_m):
            rows_all[m * kr : (m + 1) * kr, :] = basis[m].astype(F32)

    sums = pack[:, 0:1, hd + kr : hd + kr + 3].astype(F32)
    damping = jnp.sum(jnp.sum(sums, axis=0), axis=1, keepdims=True) * (DAMP_FACTOR / count)
    for i in range(per):
        turned = pack[g * per + i][:, :hd]
        grad = jnp.dot(rq_t[...], turned, preferred_element_type=F32) * (1.0 / rq.shape[1])
        eigs = eig[:, i * hd : (i + 1) * hd].astype(F32)
        scaled[:, i * hd : (i + 1) * hd] = (grad / (eigs + damping)).astype(BF)
    n = jnp.dot(rows_all[...].astype(BF), scaled[...], preferred_element_type=F32)
    for i in range(per):
        for m in range(n_m):
            out[i, m] = n[m * kr : (m + 1) * kr, i * hd : (i + 1) * hd].astype(BF)


def spread(count, rq, pack, eig, basis, hd):
    heads = pack.shape[0]
    n_m, rows, cols = basis.shape
    per = heads // 2
    return pl.pallas_call(
        functools.partial(spread_kernel, count),
        grid=(2,),
        out_shape=jax.ShapeDtypeStruct((heads, n_m, rows, hd), BF),
        in_specs=[
            *vmem(2),
            pl.BlockSpec((cols, per * hd), lambda g: (0, g)),
            *vmem(1),
        ],
        out_specs=pl.BlockSpec((per, n_m, rows, hd), lambda g: (g, 0, 0, 0)),
        scratch_shapes=[
            pltpu.VMEM((cols, rq.shape[1]), BF),
            pltpu.VMEM((n_m * rows, cols), F32),
            pltpu.VMEM((cols, per * hd), BF),
        ],
        interpret=INTERPRET,
        name="spread",
        compiler_params=limit(16),
    )(*held([rq, pack]), eig, *held([basis]))


def add_planes_kernel(x_ref, own, r1, r2, r3, out_0, out_1, out_2):
    near, mid, far = own[2].astype(F32), own[1].astype(F32), own[0].astype(F32)
    for k, ref in ((1, r1), (2, r2), (3, r3)):
        low, high = ref[0].astype(F32), ref[1].astype(F32)
        later = x_ref[0] + k < NX
        near = near + jnp.where(later, high, 0.0)
        mid = mid + jnp.where(later, low, high)
        far = far + jnp.where(later, 0.0, low)
    out_0[...] = near
    out_1[...] = mid.astype(BF)
    out_2[...] = far.astype(BF)


def add_planes(x, own, got):
    one = own.shape[1:]
    return pl.pallas_call(
        add_planes_kernel,
        out_shape=tuple(jax.ShapeDtypeStruct(one, t) for t in (F32, BF, BF)),
        in_specs=[pl.BlockSpec(memory_space=pltpu.SMEM)] + vmem(4),
        out_specs=tuple(vmem(3)),
        interpret=INTERPRET,
        name="add_planes",
        compiler_params=limit(16),
    )(x, own, *held(got))


def score_kernel(place_ref, n_ref, bg_ref, sum_0, got_1, got_2, partner, *refs):
    *mine, out = refs
    tile = out.shape[2]
    acc = None
    for i, ref in enumerate(mine):
        for at, part in ((place_ref[i], ref), (place_ref[i] ^ 1, partner.at[i])):
            term = jnp.dot(n_ref[at].T, part[...], preferred_element_type=F32)
            acc = term if acc is None else acc + term
    mapped = jnp.dot(bg_ref[...], acc.astype(BF), preferred_element_type=F32)
    adjoint = sum_0[...] + got_1[...].astype(F32) + got_2[...].astype(F32)
    total = jnp.sum(mapped * adjoint.T, axis=0, keepdims=True)
    for i in range(out.shape[1]):
        out[:, i, :] = jnp.broadcast_to(
            total[:, i * tile : (i + 1) * tile], (out.shape[0], tile)
        )


def score(place, n8, bg, sum_0, got_1, got_2, mine, partner):
    _, rows = mine[0].shape
    heads = n8.shape[0]
    tile = 128
    return pl.pallas_call(
        score_kernel,
        out_shape=jax.ShapeDtypeStruct((heads, rows // tile, tile), F32),
        in_specs=[pl.BlockSpec(memory_space=pltpu.SMEM)] + vmem(6 + len(mine)),
        out_specs=vmem(1)[0],
        interpret=INTERPRET,
        name="score",
        compiler_params=limit(16),
    )(place, *held([n8]), bg, *held([sum_0, got_1, got_2, partner, *mine]))


def on_device(
    act, query_rows, key_rows, out_adjoint, basis_input, basis_grad, eigvals, query_act, query_adj
):
    rows, cols = act.shape
    hd = basis_grad.shape[1]
    heads = lax.axis_size("head")
    n_y = heads // 2
    n_m = lax.axis_size("seq") // NX // NC
    span = WINDOW // rows
    tie = lax.optimization_barrier
    s = lax.axis_index("seq")
    h = lax.axis_index("head")
    x = s & (NX - 1)
    c = (s >> 2) & (NC - 1)
    ahead = [x + k < NX for k in range(NX)]

    key_1 = shift_z(key_rows, 1, False)
    key_2 = shift_z(key_rows, 2, False)
    basis = exchange(copies(basis_input, n_m), "seq", m_groups())
    at = (c & 1) * NX + x
    pack = pack_query(at[None], query_act, query_adj, basis_grad[0], eigvals, heads)
    act_t = act.T
    mine = [act_t] + [shift_y(act_t, j) for j in range(1, n_y)]
    key_1, key_2, basis, pack = tie((key_1, key_2, basis, pack))

    pack = exchange(pack, "head")
    pairs = []
    for k in range(1, NX):
        pair = jnp.stack([jnp.where(ahead[k], key_1, key_2), jnp.where(ahead[k], key_rows, key_1)])
        pairs.append(shift_x(pair, k))
    rq = rotate_query(c[None], pack, basis, hd)
    rq, pairs = tie((rq, pairs))

    rq = exchange(rq, "seq", x_groups())
    own, *back = attend(
        s[None], query_rows, out_adjoint, (key_2, key_1, key_rows), pairs, span
    )
    rq = copies(jnp.sum(rq.astype(F32), axis=0).astype(BF), NC)
    rq, own, back = tie((rq, own, back))
    rq = exchange(rq, "seq", c_groups())
    n = spread(float(cols * heads * eigvals.shape[1]), rq, pack, eigvals, basis, hd)
    n, back, mine = tie((n, back, mine))

    n = exchange(n, "head")
    got = [shift_x(back[k - 1], -k) for k in range(1, NX)]
    n = copies(jnp.sum(n.astype(F32), axis=0).astype(BF), NC)
    stacked = jnp.stack(mine)
    n, got, stacked = tie((n, got, stacked))

    n = exchange(n, "seq", c_groups())
    sum_0, sum_1, sum_2 = add_planes(x[None], own, got)
    got_1 = shift_z(sum_1, -1, False)
    got_2 = shift_z(sum_2, -2, False)
    n, stacked = tie((n, stacked))
    n = exchange(copies(n, NX), "seq", x_groups())
    partner = lax.ppermute(stacked, "head", [(i, i ^ 1) for i in range(heads)])
    n = n.transpose(2, 1, 0, 3, 4).reshape(heads, cols, hd)
    place = (h + 2 * (n_y - jnp.arange(n_y, dtype=jnp.int32))) & (heads - 1)
    partial = score(place, n, basis_grad[0], sum_0, got_1, got_2, mine, partner)
    partial = exchange(partial, "head")
    return jnp.sum(partial, axis=0).reshape(rows)


def solution(mesh):
    return jax.shard_map(
        on_device,
        mesh=mesh,
        in_specs=(
            P("seq", "head"),
            P("seq", "head"),
            P("seq", "head"),
            P("seq", "head"),
            P("seq", "head"),
            P("head", None, None),
            P("head", None),
            P(None, "head"),
            P(None, "head"),
        ),
        out_specs=P("seq"),
        check_vma=False,
    )
```

```python
import functools

import jax
import jax.numpy as jnp
from jax import lax
from jax.experimental import pallas as pl
from jax.experimental.pallas import tpu as pltpu
from jax.sharding import PartitionSpec as P


WINDOW = 4096
SCORE_SCALE = 1.0 / 12.0
SOFT_CAP = 50.0
DAMP_FACTOR = 0.1
LOG2E = 1.4426950408889634
NX = 4
NC = 4
BF = jnp.bfloat16
F32 = jnp.float32
NT = (((1,), (1,)), ((), ()))
INTERPRET = False


def vmem(n):
    return [pl.BlockSpec(memory_space=pltpu.VMEM) for _ in range(n)]


def held(values):
    return [pltpu.with_memory_space_constraint(v, pltpu.VMEM) for v in values]


def limit(mib):
    return pltpu.CompilerParams(vmem_limit_bytes=mib << 20)


def shift_z(value, by, wrap):
    size = lax.axis_size("seq")
    pairs = [(i, (i + by * NX) % size) for i in range(size) if wrap or 0 <= i + by * NX < size]
    return lax.ppermute(value, "seq", pairs)


def shift_x(value, by):
    size = lax.axis_size("seq")
    pairs = [(i, i // NX * NX + (i % NX + by) % NX) for i in range(size)]
    return lax.ppermute(value, "seq", pairs)


def shift_y(value, by):
    size = lax.axis_size("head")
    return lax.ppermute(value, "head", [(i, (i + 2 * by) % size) for i in range(size)])


def x_groups():
    size = lax.axis_size("seq")
    return [[z * NX + x for x in range(NX)] for z in range(size // NX)]


def c_groups():
    size = lax.axis_size("seq")
    return [
        [(b * NC + c) * NX + x for c in range(NC)]
        for b in range(size // NX // NC)
        for x in range(NX)
    ]


def exchange(value, axis, groups=None):
    return lax.all_to_all(value, axis, 0, 0, axis_index_groups=groups)


def copies(value, count):
    return jnp.broadcast_to(value[None], (count,) + value.shape)


def attend_kernel(span, s_ref, q_ref, a_ref, z2, z1, z0, p1, p2, p3, own, b1, b2, b3, kbuf, w, tot, adjt):
    rows, hd = z0.shape
    s = s_ref[0]
    pairs = (p1, p2, p3)
    kbuf[0] = z0[...]
    kbuf[4] = z1[...]
    kbuf[8] = z2[...]
    for k in range(1, 4):
        kbuf[k + 4] = pairs[k - 1][0]
        kbuf[k] = pairs[k - 1][1]
    tot[...] = jnp.zeros_like(tot)
    half = rows // 2

    def block(o, mode):
        for piece in range(2):
            lo = piece * half
            keys = kbuf[o, lo : lo + half, :]
            for m in range(2):
                raw = lax.dot_general(
                    keys, q_ref[:, m * hd : (m + 1) * hd], NT, preferred_element_type=F32
                )
                e = jnp.exp2(jnp.tanh(raw * (SCORE_SCALE / SOFT_CAP)) * (SOFT_CAP * LOG2E))
                if mode != 0:
                    key_i = lo + lax.broadcasted_iota(jnp.int32, e.shape, 0)
                    query_i = lax.broadcasted_iota(jnp.int32, e.shape, 1)
                    keep = key_i <= query_i if mode < 0 else key_i > query_i
                    e = jnp.where(keep, e, 0.0)
                tot[m] += jnp.sum(e.reshape(half // 8, 8, rows), axis=0)
                w[o, lo : lo + half, m * rows : (m + 1) * rows] = e.astype(BF)

    block(0, -1)

    def step(o, carry):
        block(o, 0)
        return carry

    lax.fori_loop(1, jnp.minimum(s, span - 1) + 1, step, 0)

    @pl.when(s >= span)
    def _():
        block(span, 1)

    @pl.when(s < span)
    def _():
        def clear(o, carry):
            w[o] = jnp.zeros(w.shape[1:], BF)
            return carry

        lax.fori_loop(s + 1, span + 1, clear, 0)

    for m in range(2):
        inv = 1.0 / jnp.sum(tot[m], axis=0, keepdims=True)
        turned = a_ref[:, m * hd : (m + 1) * hd].astype(F32).T
        adjt[:, m * rows : (m + 1) * rows] = (turned * inv).astype(BF)
    for o in range(span + 1):
        piece = lax.dot_general(w[o], adjt[...], NT, preferred_element_type=F32).astype(BF)
        if o % 4 == 0:
            own[2 - o // 4] = piece
        else:
            (b1, b2, b3)[o % 4 - 1][1 - o // 4] = piece


def attend(s, q, a, keys, pairs, span):
    rows, hd = keys[0].shape
    pair = jax.ShapeDtypeStruct((2, rows, hd), BF)
    return pl.pallas_call(
        functools.partial(attend_kernel, span),
        out_shape=(jax.ShapeDtypeStruct((3, rows, hd), BF), pair, pair, pair),
        in_specs=[pl.BlockSpec(memory_space=pltpu.SMEM)] + vmem(8),
        out_specs=tuple(vmem(4)),
        scratch_shapes=[
            pltpu.VMEM((span + 1, rows, hd), BF),
            pltpu.VMEM((span + 1, rows, 2 * rows), BF),
            pltpu.VMEM((2, 8, rows), F32),
            pltpu.VMEM((hd, 2 * rows), BF),
        ],
        interpret=INTERPRET,
        name="attend",
    )(s, q, a, *keys, *pairs)


def pack_kernel(at_ref, act, adj, bg, eig, out):
    lq, hd = adj.shape
    heads = out.shape[0]
    kr = act.shape[1] // heads
    turned = jnp.dot(adj[...], bg[...], preferred_element_type=F32).astype(BF)
    total = jnp.sum(jnp.sum(eig[...].astype(F32), axis=0, keepdims=True), axis=1, keepdims=True)
    high = total.astype(BF).astype(F32)
    mid = (total - high).astype(BF).astype(F32)
    low = total - high - mid
    lane = lax.broadcasted_iota(jnp.int32, (lq, hd - kr), 1)
    tail = jnp.where(lane == 0, high, jnp.where(lane == 1, mid, jnp.where(lane == 2, low, 0.0)))
    out[0, :, :hd] = turned
    out[0, :, hd + kr :] = tail.astype(BF)
    for i in range(heads):

        @pl.when(at_ref[0] == i)
        def _():
            out[0, :, hd : hd + kr] = act[:, i * kr : (i + 1) * kr]

    for i in range(1, heads):
        out[i] = out[0]


def pack_query(at, act, adj, bg, eig, heads):
    lq, hd = adj.shape
    return pl.pallas_call(
        pack_kernel,
        out_shape=jax.ShapeDtypeStruct((heads, lq, 2 * hd), BF),
        in_specs=[pl.BlockSpec(memory_space=pltpu.SMEM)] + vmem(4),
        out_specs=vmem(1)[0],
        interpret=INTERPRET,
        name="pack_query",
    )(at, act, adj, bg, eig)


def rotate_query_kernel(hd, h_ref, pack, *refs):
    *basis, out = refs
    acc = None
    for j, block in enumerate(basis):
        chunk = pack[h_ref[j]][:, hd : hd + block.shape[0]]
        term = jnp.dot(chunk, block[...], preferred_element_type=F32)
        acc = term if acc is None else acc + term
    acc = acc.astype(BF)
    for i in range(out.shape[0]):
        out[i] = acc


def rotate_query(h_index, pack, basis, hd):
    return pl.pallas_call(
        functools.partial(rotate_query_kernel, hd),
        out_shape=jax.ShapeDtypeStruct((NX, pack.shape[1], basis[0].shape[1]), BF),
        in_specs=[pl.BlockSpec(memory_space=pltpu.SMEM)] + vmem(1 + len(basis)),
        out_specs=vmem(1)[0],
        interpret=INTERPRET,
        name="rotate_query",
    )(h_index, pack, *basis)


def spread_kernel(count, rq, pack, eig, *refs):
    *basis, out, rq_t, rows_all, scaled = refs
    hd = out.shape[3]
    kr, _ = basis[0].shape
    per = out.shape[0]
    g = pl.program_id(0)

    @pl.when(g == 0)
    def _():
        total = rq[0].astype(F32)
        for i in range(1, rq.shape[0]):
            total = total + rq[i].astype(F32)
        rq_t[...] = total.T.astype(BF)
        for j, block in enumerate(basis):
            rows_all[j * kr : (j + 1) * kr, :] = block[...].astype(F32)

    sums = pack[:, 0:1, hd + kr : hd + kr + 3].astype(F32)
    damping = jnp.sum(jnp.sum(sums, axis=0), axis=1, keepdims=True) * (DAMP_FACTOR / count)
    for i in range(per):
        turned = pack[g * per + i][:, :hd]
        grad = jnp.dot(rq_t[...], turned, preferred_element_type=F32) * (1.0 / rq.shape[1])
        eigs = eig[:, i * hd : (i + 1) * hd].astype(F32)
        scaled[:, i * hd : (i + 1) * hd] = (grad / (eigs + damping)).astype(BF)
    n = jnp.dot(rows_all[...].astype(BF), scaled[...], preferred_element_type=F32)
    for i in range(per):
        for j in range(len(basis)):
            out[i, j] = n[j * kr : (j + 1) * kr, i * hd : (i + 1) * hd].astype(BF)


def spread(count, rq, pack, eig, basis, hd):
    heads = pack.shape[0]
    n_m = len(basis)
    rows, cols = basis[0].shape
    per = heads // 2
    return pl.pallas_call(
        functools.partial(spread_kernel, count),
        grid=(2,),
        out_shape=jax.ShapeDtypeStruct((heads, n_m, rows, hd), BF),
        in_specs=[
            *vmem(1),
            pl.BlockSpec(pack.shape, lambda g: (0, 0, 0)),
            pl.BlockSpec((cols, per * hd), lambda g: (0, g)),
        ]
        + [pl.BlockSpec((rows, cols), lambda g: (0, 0)) for _ in basis],
        out_specs=pl.BlockSpec((per, n_m, rows, hd), lambda g: (g, 0, 0, 0)),
        scratch_shapes=[
            pltpu.VMEM((cols, rq.shape[1]), BF),
            pltpu.VMEM((n_m * rows, cols), F32),
            pltpu.VMEM((cols, per * hd), BF),
        ],
        interpret=INTERPRET,
        name="spread",
    )(*held([rq]), pack, eig, *basis)


def add_planes_kernel(x_ref, own, r1, r2, r3, out_0, out_1, out_2):
    near, mid, far = own[2].astype(F32), own[1].astype(F32), own[0].astype(F32)
    for k, ref in ((1, r1), (2, r2), (3, r3)):
        low, high = ref[0].astype(F32), ref[1].astype(F32)
        later = x_ref[0] + k < NX
        near = near + jnp.where(later, high, 0.0)
        mid = mid + jnp.where(later, low, high)
        far = far + jnp.where(later, 0.0, low)
    out_0[...] = near
    out_1[...] = mid.astype(BF)
    out_2[...] = far.astype(BF)


def add_planes(x, own, got):
    one = own.shape[1:]
    return pl.pallas_call(
        add_planes_kernel,
        out_shape=tuple(jax.ShapeDtypeStruct(one, t) for t in (F32, BF, BF)),
        in_specs=[pl.BlockSpec(memory_space=pltpu.SMEM)] + vmem(4),
        out_specs=tuple(vmem(3)),
        interpret=INTERPRET,
        name="add_planes",
    )(x, own, *held(got))


def score_kernel(place_ref, n_ref, bg_ref, sum_0, got_1, got_2, partner, *refs):
    *mine, out = refs
    tile = out.shape[2]
    acc = None
    for i, ref in enumerate(mine):
        for at, part in ((place_ref[i], ref), (place_ref[i] ^ 1, partner.at[i])):
            term = jnp.dot(n_ref[at].T, part[...], preferred_element_type=F32)
            acc = term if acc is None else acc + term
    mapped = jnp.dot(bg_ref[...], acc.astype(BF), preferred_element_type=F32)
    adjoint = sum_0[...] + got_1[...].astype(F32) + got_2[...].astype(F32)
    total = jnp.sum(mapped * adjoint.T, axis=0, keepdims=True)
    for i in range(out.shape[1]):
        out[:, i, :] = jnp.broadcast_to(
            total[:, i * tile : (i + 1) * tile], (out.shape[0], tile)
        )


def score(place, n8, bg, sum_0, got_1, got_2, mine, partner):
    _, rows = mine[0].shape
    heads = n8.shape[0]
    tile = 128
    return pl.pallas_call(
        score_kernel,
        out_shape=jax.ShapeDtypeStruct((heads, rows // tile, tile), F32),
        in_specs=[pl.BlockSpec(memory_space=pltpu.SMEM)] + vmem(6 + len(mine)),
        out_specs=vmem(1)[0],
        interpret=INTERPRET,
        name="score",
        compiler_params=limit(16),
    )(place, *held([n8]), bg, *held([sum_0, got_1, got_2, partner, *mine]))


def on_device(
    act, query_rows, key_rows, out_adjoint, basis_input, basis_grad, eigvals, query_act, query_adj
):
    rows, cols = act.shape
    hd = basis_grad.shape[1]
    heads = lax.axis_size("head")
    n_y = heads // 2
    n_m = lax.axis_size("seq") // NX // NC
    span = WINDOW // rows
    tie = lax.optimization_barrier
    s = lax.axis_index("seq")
    h = lax.axis_index("head")
    x = s & (NX - 1)
    z = s >> 2
    c = z & (NC - 1)
    ahead = [x + k < NX for k in range(NX)]
    j = jnp.arange(n_m, dtype=jnp.int32)

    key_1 = shift_z(key_rows, 1, False)
    key_2 = shift_z(key_rows, 2, False)
    at = (c & 1) * NX + x
    pack = pack_query(at[None], query_act, query_adj, basis_grad[0], eigvals, heads)
    pack = exchange(pack, "head")
    basis = [basis_input] + [shift_z(basis_input, -NC * i, True) for i in range(1, n_m)]
    h_index = ((z + NC * j) & (n_m * NC - 1)) >> 1
    rq = rotate_query(h_index, pack, basis, hd)
    rq, key_1, key_2 = tie((rq, key_1, key_2))

    rq = exchange(rq, "seq", x_groups())
    pairs = []
    for k in range(1, NX):
        pair = jnp.stack([jnp.where(ahead[k], key_1, key_2), jnp.where(ahead[k], key_rows, key_1)])
        pairs.append(shift_x(pair, k))
    rq = copies(jnp.sum(rq.astype(F32), axis=0).astype(BF), NC)
    rq = exchange(rq, "seq", c_groups())
    act_t = act.T
    mine = [act_t] + [shift_y(act_t, i) for i in range(1, n_y)]
    pairs = tie(pairs)
    own, *back = attend(
        s[None], query_rows, out_adjoint, (key_2, key_1, key_rows), pairs, span
    )
    rq, own, back = tie((rq, own, back))

    n = spread(float(cols * heads * eigvals.shape[1]), rq, pack, eigvals, basis, hd)
    n = exchange(n, "head")
    got = [shift_x(back[k - 1], -k) for k in range(1, NX)]
    n = copies(jnp.sum(n.astype(F32), axis=0).astype(BF), NC)
    stacked = jnp.stack(mine)
    n = exchange(n, "seq", c_groups())
    sum_0, sum_1, sum_2 = add_planes(x[None], own, got)
    got_1 = shift_z(sum_1, -1, False)
    got_2 = shift_z(sum_2, -2, False)
    n = exchange(copies(n, NX), "seq", x_groups())
    partner = lax.ppermute(stacked, "head", [(i, i ^ 1) for i in range(heads)])
    n = n.transpose(2, 1, 0, 3, 4).reshape(heads, cols, hd)
    of = (h + 2 * (n_y - jnp.arange(n_y, dtype=jnp.int32))) & (heads - 1)
    place = 2 * (((of >> 1) - (z >> 2)) & (n_m - 1)) + (of & 1)
    partial = score(place, n, basis_grad[0], sum_0, got_1, got_2, mine, partner)
    partial = exchange(partial, "head")
    return jnp.sum(partial, axis=0).reshape(rows)


def solution(mesh):
    return jax.shard_map(
        on_device,
        mesh=mesh,
        in_specs=(
            P("seq", "head"),
            P("seq", "head"),
            P("seq", "head"),
            P("seq", "head"),
            P("seq", "head"),
            P("head", None, None),
            P("head", None),
            P(None, "head"),
            P(None, "head"),
        ),
        out_specs=P("seq"),
        check_vma=False,
    )
```

```python
import functools

import jax
import jax.numpy as jnp
from jax import lax
from jax.experimental import pallas as pl
from jax.experimental.pallas import tpu as pltpu
from jax.sharding import PartitionSpec as P


WINDOW = 4096
SCORE_SCALE = 1.0 / 12.0
SOFT_CAP = 50.0
DAMP_FACTOR = 0.1
LOG2E = 1.4426950408889634
NX = 4
NC = 4
BF = jnp.bfloat16
F32 = jnp.float32
NT = (((1,), (1,)), ((), ()))
INTERPRET = False


def vmem(n):
    return [pl.BlockSpec(memory_space=pltpu.VMEM) for _ in range(n)]


def held(values):
    return [pltpu.with_memory_space_constraint(v, pltpu.VMEM) for v in values]


def limit(mib):
    return pltpu.CompilerParams(vmem_limit_bytes=mib << 20)


def shift_z(value, by, wrap):
    size = lax.axis_size("seq")
    pairs = [(i, (i + by * NX) % size) for i in range(size) if wrap or 0 <= i + by * NX < size]
    return lax.ppermute(value, "seq", pairs)


def shift_x(value, by):
    size = lax.axis_size("seq")
    pairs = [(i, i // NX * NX + (i % NX + by) % NX) for i in range(size)]
    return lax.ppermute(value, "seq", pairs)


def shift_y(value, by):
    size = lax.axis_size("head")
    return lax.ppermute(value, "head", [(i, (i + 2 * by) % size) for i in range(size)])


def x_groups():
    size = lax.axis_size("seq")
    return [[z * NX + x for x in range(NX)] for z in range(size // NX)]


def c_groups():
    size = lax.axis_size("seq")
    return [
        [(b * NC + c) * NX + x for c in range(NC)]
        for b in range(size // NX // NC)
        for x in range(NX)
    ]


def exchange(value, axis, groups=None):
    return lax.all_to_all(value, axis, 0, 0, axis_index_groups=groups)


def copies(value, count):
    return jnp.broadcast_to(value[None], (count,) + value.shape)


def attend_kernel(span, s_ref, q_ref, a_ref, z2, z1, z0, p1, p2, p3, own, b1, b2, b3, kbuf, w, tot, adjt):
    rows, hd = z0.shape
    s = s_ref[0]
    pairs = (p1, p2, p3)
    kbuf[0] = z0[...]
    kbuf[4] = z1[...]
    kbuf[8] = z2[...]
    for k in range(1, 4):
        kbuf[k + 4] = pairs[k - 1][0]
        kbuf[k] = pairs[k - 1][1]
    tot[...] = jnp.zeros_like(tot)
    half = rows // 2

    def block(o, mode):
        for piece in range(2):
            lo = piece * half
            keys = kbuf[o, lo : lo + half, :]
            for m in range(2):
                raw = lax.dot_general(
                    keys, q_ref[:, m * hd : (m + 1) * hd], NT, preferred_element_type=F32
                )
                e = jnp.exp2(jnp.tanh(raw * (SCORE_SCALE / SOFT_CAP)) * (SOFT_CAP * LOG2E))
                if mode != 0:
                    key_i = lo + lax.broadcasted_iota(jnp.int32, e.shape, 0)
                    query_i = lax.broadcasted_iota(jnp.int32, e.shape, 1)
                    keep = key_i <= query_i if mode < 0 else key_i > query_i
                    e = jnp.where(keep, e, 0.0)
                tot[m] += jnp.sum(e.reshape(half // 8, 8, rows), axis=0)
                w[o, lo : lo + half, m * rows : (m + 1) * rows] = e.astype(BF)

    block(0, -1)

    def step(o, carry):
        block(o, 0)
        return carry

    lax.fori_loop(1, jnp.minimum(s, span - 1) + 1, step, 0)

    @pl.when(s >= span)
    def _():
        block(span, 1)

    @pl.when(s < span)
    def _():
        def clear(o, carry):
            w[o] = jnp.zeros(w.shape[1:], BF)
            return carry

        lax.fori_loop(s + 1, span + 1, clear, 0)

    for m in range(2):
        inv = 1.0 / jnp.sum(tot[m], axis=0, keepdims=True)
        turned = a_ref[:, m * hd : (m + 1) * hd].astype(F32).T
        adjt[:, m * rows : (m + 1) * rows] = (turned * inv).astype(BF)
    for o in range(span + 1):
        piece = lax.dot_general(w[o], adjt[...], NT, preferred_element_type=F32).astype(BF)
        if o % 4 == 0:
            own[2 - o // 4] = piece
        else:
            (b1, b2, b3)[o % 4 - 1][1 - o // 4] = piece


def attend(s, q, a, keys, pairs, span):
    rows, hd = keys[0].shape
    pair = jax.ShapeDtypeStruct((2, rows, hd), BF)
    return pl.pallas_call(
        functools.partial(attend_kernel, span),
        out_shape=(jax.ShapeDtypeStruct((3, rows, hd), BF), pair, pair, pair),
        in_specs=[pl.BlockSpec(memory_space=pltpu.SMEM)] + vmem(8),
        out_specs=tuple(vmem(4)),
        scratch_shapes=[
            pltpu.VMEM((span + 1, rows, hd), BF),
            pltpu.VMEM((span + 1, rows, 2 * rows), BF),
            pltpu.VMEM((2, 8, rows), F32),
            pltpu.VMEM((hd, 2 * rows), BF),
        ],
        interpret=INTERPRET,
        name="attend",
    )(s, q, a, *keys, *pairs)


def pack_kernel(at_ref, act, adj, bg, eig, out):
    lq, hd = adj.shape
    heads = out.shape[0]
    kr = act.shape[1] // heads
    turned = jnp.dot(adj[...], bg[...], preferred_element_type=F32).astype(BF)
    total = jnp.sum(jnp.sum(eig[...].astype(F32), axis=0, keepdims=True), axis=1, keepdims=True)
    high = total.astype(BF).astype(F32)
    mid = (total - high).astype(BF).astype(F32)
    low = total - high - mid
    lane = lax.broadcasted_iota(jnp.int32, (lq, hd - kr), 1)
    tail = jnp.where(lane == 0, high, jnp.where(lane == 1, mid, jnp.where(lane == 2, low, 0.0)))
    out[0, :, :hd] = turned
    out[0, :, hd + kr :] = tail.astype(BF)
    for i in range(heads):

        @pl.when(at_ref[0] == i)
        def _():
            out[0, :, hd : hd + kr] = act[:, i * kr : (i + 1) * kr]

    for i in range(1, heads):
        out[i] = out[0]


def pack_query(at, act, adj, bg, eig, heads):
    lq, hd = adj.shape
    return pl.pallas_call(
        pack_kernel,
        out_shape=jax.ShapeDtypeStruct((heads, lq, 2 * hd), BF),
        in_specs=[pl.BlockSpec(memory_space=pltpu.SMEM)] + vmem(4),
        out_specs=vmem(1)[0],
        interpret=INTERPRET,
        name="pack_query",
    )(at, act, adj, bg, eig)


def rotate_query_kernel(s_ref, pack, *refs):
    *basis, out, turned, rows_all, damp, wide = refs
    hd = turned.shape[2]
    kr = basis[0].shape[0]
    z = s_ref[0] >> 2
    n_z = NC * len(basis)
    acc = None
    for j, block in enumerate(basis):
        chunk = pack[((z + NC * j) & (n_z - 1)) >> 1][:, hd : hd + kr]
        term = jnp.dot(chunk, block[...], preferred_element_type=F32)
        acc = term if acc is None else acc + term
        wide[j * kr : (j + 1) * kr, :] = block[...].astype(F32)
    acc = acc.astype(BF)
    for i in range(out.shape[0]):
        out[i] = acc
    turned[...] = pack[:, :, :hd]
    rows_all[...] = wide[...].astype(BF)
    sums = jnp.sum(pack[:, 0:1, hd + kr : hd + kr + 3].astype(F32), axis=0)
    damp[...] = jnp.broadcast_to(jnp.sum(sums, axis=1, keepdims=True), damp.shape)


def rotate_query(s, pack, basis, hd):
    heads, lq, _ = pack.shape
    kr, cols = basis[0].shape
    total = kr * len(basis)
    return pl.pallas_call(
        rotate_query_kernel,
        out_shape=(
            jax.ShapeDtypeStruct((NX, lq, cols), BF),
            jax.ShapeDtypeStruct((heads, lq, hd), BF),
            jax.ShapeDtypeStruct((total, cols), BF),
            jax.ShapeDtypeStruct((8, hd), F32),
        ),
        in_specs=[pl.BlockSpec(memory_space=pltpu.SMEM)] + vmem(1 + len(basis)),
        out_specs=tuple(vmem(4)),
        scratch_shapes=[pltpu.VMEM((total, cols), F32)],
        interpret=INTERPRET,
        name="rotate_query",
    )(s, *held([pack]), basis[0], *held(basis[1:]))


def spread_kernel(count, rq, turned, eig, rows_all, damp, out, rq_t, scaled):
    hd = out.shape[3]
    n_m, kr = out.shape[1:3]
    per = out.shape[0]

    @pl.when(pl.program_id(0) == 0)
    def _():
        total = rq[0].astype(F32)
        for i in range(1, rq.shape[0]):
            total = total + rq[i].astype(F32)
        rq_t[...] = total.T.astype(BF)

    damping = damp[0:1, :] * (DAMP_FACTOR / count)
    for i in range(per):
        grad = jnp.dot(rq_t[...], turned[i], preferred_element_type=F32) * (1.0 / rq.shape[1])
        eigs = eig[:, i * hd : (i + 1) * hd].astype(F32)
        scaled[:, i * hd : (i + 1) * hd] = (grad / (eigs + damping)).astype(BF)
    n = jnp.dot(rows_all[...], scaled[...], preferred_element_type=F32)
    for i in range(per):
        for j in range(n_m):
            out[i, j] = n[j * kr : (j + 1) * kr, i * hd : (i + 1) * hd].astype(BF)


def spread(count, rq, turned, eig, rows_all, damp, n_m):
    heads, lq, hd = turned.shape
    total, cols = rows_all.shape
    rows = total // n_m
    per = heads // 2
    return pl.pallas_call(
        functools.partial(spread_kernel, count),
        grid=(2,),
        out_shape=jax.ShapeDtypeStruct((heads, n_m, rows, hd), BF),
        in_specs=[
            *vmem(1),
            pl.BlockSpec((per, lq, hd), lambda g: (g, 0, 0)),
            pl.BlockSpec((cols, per * hd), lambda g: (0, g)),
            pl.BlockSpec((total, cols), lambda g: (0, 0)),
            pl.BlockSpec(damp.shape, lambda g: (0, 0)),
        ],
        out_specs=pl.BlockSpec((per, n_m, rows, hd), lambda g: (g, 0, 0, 0)),
        scratch_shapes=[
            pltpu.VMEM((cols, lq), BF),
            pltpu.VMEM((cols, per * hd), BF),
        ],
        interpret=INTERPRET,
        name="spread",
    )(*held([rq]), turned, eig, rows_all, damp)


def sum_copies_kernel(a_ref, out):
    total = a_ref[0].astype(F32)
    for i in range(1, a_ref.shape[0]):
        total = total + a_ref[i].astype(F32)
    total = total.astype(BF)
    for i in range(out.shape[0]):
        out[i] = total


def sum_copies(a, count):
    return pl.pallas_call(
        sum_copies_kernel,
        out_shape=jax.ShapeDtypeStruct((count,) + a.shape[1:], BF),
        in_specs=vmem(1),
        out_specs=vmem(1)[0],
        interpret=INTERPRET,
        name="sum_copies",
    )(*held([a]))


def add_planes_kernel(x_ref, own, r1, r2, r3, out_0, out_1, out_2):
    near, mid, far = own[2].astype(F32), own[1].astype(F32), own[0].astype(F32)
    for k, ref in ((1, r1), (2, r2), (3, r3)):
        low, high = ref[0].astype(F32), ref[1].astype(F32)
        later = x_ref[0] + k < NX
        near = near + jnp.where(later, high, 0.0)
        mid = mid + jnp.where(later, low, high)
        far = far + jnp.where(later, 0.0, low)
    out_0[...] = near
    out_1[...] = mid.astype(BF)
    out_2[...] = far.astype(BF)


def add_planes(x, own, got):
    one = own.shape[1:]
    return pl.pallas_call(
        add_planes_kernel,
        out_shape=tuple(jax.ShapeDtypeStruct(one, t) for t in (F32, BF, BF)),
        in_specs=[pl.BlockSpec(memory_space=pltpu.SMEM)] + vmem(4),
        out_specs=tuple(vmem(3)),
        interpret=INTERPRET,
        name="add_planes",
    )(x, own, *held(got))


def score_kernel(place_ref, n_ref, bg_ref, sum_0, got_1, got_2, partner, *refs):
    *mine, out = refs
    tile = out.shape[2]
    acc = None
    for i, ref in enumerate(mine):
        for at, part in ((place_ref[i], ref), (place_ref[i] ^ 1, partner.at[i])):
            term = jnp.dot(n_ref[at].T, part[...], preferred_element_type=F32)
            acc = term if acc is None else acc + term
    mapped = jnp.dot(bg_ref[...], acc.astype(BF), preferred_element_type=F32)
    adjoint = sum_0[...] + got_1[...].astype(F32) + got_2[...].astype(F32)
    total = jnp.sum(mapped * adjoint.T, axis=0, keepdims=True)
    for i in range(out.shape[1]):
        out[:, i, :] = jnp.broadcast_to(
            total[:, i * tile : (i + 1) * tile], (out.shape[0], tile)
        )


def score(place, n8, bg, sum_0, got_1, got_2, mine, partner):
    _, rows = mine[0].shape
    heads = n8.shape[0]
    tile = 128
    return pl.pallas_call(
        score_kernel,
        out_shape=jax.ShapeDtypeStruct((heads, rows // tile, tile), F32),
        in_specs=[pl.BlockSpec(memory_space=pltpu.SMEM)] + vmem(6 + len(mine)),
        out_specs=vmem(1)[0],
        interpret=INTERPRET,
        name="score",
        compiler_params=limit(16),
    )(place, *held([n8]), bg, *held([sum_0, got_1, got_2, partner, *mine]))


def on_device(
    act, query_rows, key_rows, out_adjoint, basis_input, basis_grad, eigvals, query_act, query_adj
):
    rows, cols = act.shape
    hd = basis_grad.shape[1]
    heads = lax.axis_size("head")
    n_y = heads // 2
    n_m = lax.axis_size("seq") // NX // NC
    span = WINDOW // rows
    tie = lax.optimization_barrier
    s = lax.axis_index("seq")
    h = lax.axis_index("head")
    x = s & (NX - 1)
    z = s >> 2
    c = z & (NC - 1)
    ahead = [x + k < NX for k in range(NX)]

    key_1 = shift_z(key_rows, 1, False)
    key_2 = shift_z(key_rows, 2, False)
    at = (c & 1) * NX + x
    pack = pack_query(at[None], query_act, query_adj, basis_grad[0], eigvals, heads)
    pack = exchange(pack, "head")
    basis = [basis_input] + [shift_z(basis_input, -NC * i, True) for i in range(1, n_m)]
    rq, turned, rows_all, damp = rotate_query(s[None], pack, basis, hd)
    rq, key_1, key_2 = tie((rq, key_1, key_2))

    rq = exchange(rq, "seq", x_groups())
    pairs = []
    for k in range(1, NX):
        pair = jnp.stack([jnp.where(ahead[k], key_1, key_2), jnp.where(ahead[k], key_rows, key_1)])
        pairs.append(shift_x(pair, k))
    rq = copies(jnp.sum(rq.astype(F32), axis=0).astype(BF), NC)
    rq = exchange(rq, "seq", c_groups())
    act_t = act.T
    mine = [act_t, shift_y(act_t, 1)]
    mine = mine + [shift_y(act_t, i) for i in range(2, n_y)]
    pairs = tie(pairs)
    own, *back = attend(
        s[None], query_rows, out_adjoint, (key_2, key_1, key_rows), pairs, span
    )

    count = float(cols * heads * eigvals.shape[1])
    n = spread(count, rq, turned, eigvals, rows_all, damp, n_m)
    n = exchange(n, "head")
    got = [shift_x(back[k - 1], -k) for k in range(1, NX)]
    n = sum_copies(n, NC)
    stacked = jnp.stack(mine)
    n = exchange(n, "seq", c_groups())
    sum_0, sum_1, sum_2 = add_planes(x[None], own, got)
    got_1 = shift_z(sum_1, -1, False)
    got_2 = shift_z(sum_2, -2, False)
    n = exchange(copies(n, NX), "seq", x_groups())
    partner = lax.ppermute(stacked, "head", [(i, i ^ 1) for i in range(heads)])
    n = n.transpose(2, 1, 0, 3, 4).reshape(heads, cols, hd)
    of = (h + 2 * (n_y - jnp.arange(n_y, dtype=jnp.int32))) & (heads - 1)
    place = 2 * (((of >> 1) - (z >> 2)) & (n_m - 1)) + (of & 1)
    partial = score(place, n, basis_grad[0], sum_0, got_1, got_2, mine, partner)
    partial = exchange(partial, "head")
    return jnp.sum(partial, axis=0).reshape(rows)


def solution(mesh):
    return jax.shard_map(
        on_device,
        mesh=mesh,
        in_specs=(
            P("seq", "head"),
            P("seq", "head"),
            P("seq", "head"),
            P("seq", "head"),
            P("seq", "head"),
            P("head", None, None),
            P("head", None),
            P(None, "head"),
            P(None, "head"),
        ),
        out_specs=P("seq"),
        check_vma=False,
    )
```
